32 devices in a mesh: leaf: 4 (over y, x), front: 8 (over z, core).
Axes of the slice: x: 2, y: 2, z: 4, core: 2. Of those that a mesh axis runs over, the one named last changes fastest.
Arguments:
- probe_seeds: int32 [32], replicated, may hold values from 0 to 32748
- leaf_inverse: bfloat16 [4, 1024, 1024], P('leaf', 'front'), as said below
- leaf_update: bfloat16 [4, 1024, 4096], P('leaf', 'front'), may hold values from -0.09375 to 0.09375
- internal_inverse: bfloat16 [4, 1024, 1024], P('leaf', 'front'), as said below
- internal_update: bfloat16 [4, 1024, 4096], P('leaf', 'front'), may hold values from -0.09375 to 0.09375
- child_map: int32 [4, 2, 64], P('leaf'), may hold values from 0 to 80, as said below
Outputs:
- leaf_solution: float32 [4, 32, 1024], P('leaf', None, 'front')
- internal_solution: float32 [4, 32, 1024], P('leaf', None, 'front')
The draws below stay inside these ranges and needn't reach their ends.
Inputs may be any that keep to these rules, and one draw needn't show every extreme that they name: `child_map`: in each row of a slot and child the entries other than 80 are distinct; the last row is not read. `leaf_inverse`: each supernode's matrix is lower triangular with a positive diagonal. `internal_inverse`: each slot's matrix is lower triangular with a positive diagonal.
All inputs are finite; a program needn't handle non-finite values.
Results may differ from the reference program's by a relative error of at most 0.0065.
Values may be sent and summed in bfloat16 or wider, within the bound.
No kernel may reach another device: no remote copies, remote signals or barrier semaphores. Data moves between devices by JAX's collectives and lax.ppermute only.
A program may use at most 64 MiB of HBM per device.

```python
import math
import jax
import jax.numpy as jnp
import numpy as np
from jax import lax

BLOCK = 64
PROBES = 32
LEAVES = 4
NB = 16
UPD = 64
COLS = 1024


def lower_factor(key):
    diag_key, below_key = jax.random.split(key)
    diagonal = jnp.exp(jax.random.uniform(diag_key, (LEAVES, COLS), jnp.float32, math.log(0.5), math.log(2.0)))
    below = jax.random.normal(below_key, (LEAVES, COLS, COLS), jnp.float32)
    positions = jnp.arange(COLS, dtype=jnp.int32)
    strictly = positions[:, None] > positions[None, :]
    equal_pos = positions[:, None] == positions[None, :]
    scaled = jnp.where(strictly[None, :, :], below * (1.0 / math.sqrt(COLS)), 0.0)
    full_matrix = scaled + jnp.where(equal_pos[None, :, :], diagonal[:, :, None], 0.0)
    return full_matrix.astype(jnp.bfloat16)


def draw_leaf_inverse(key, part):
    return lower_factor(jax.random.fold_in(key, 5))


def draw_internal_inverse(key, part):
    return lower_factor(jax.random.fold_in(key, 11))


def draw_child_map(key, part):
    score_key, blank_key = jax.random.split(jax.random.fold_in(key, 17))
    front_blocks = NB + UPD
    scores = jax.random.randint(score_key, (LEAVES, 2, front_blocks), 0, 1 << 20, dtype=jnp.int32)
    scores = scores * front_blocks + jnp.arange(front_blocks, dtype=jnp.int32)[None, None, :]
    ordering = jnp.argsort(scores, axis=-1, stable=True)[:, :, :UPD].astype(jnp.int32)
    blanks = jax.random.randint(blank_key, (LEAVES, 2, UPD), 0, 4, dtype=jnp.int32) == 0
    return jnp.where(blanks, front_blocks, ordering).astype(jnp.int32)


def touch_ends(entries, rng, smallest, top_value):
    index_at = [jax.random.randint(jax.random.fold_in(rng, axis), (), 0, length) for axis, length in enumerate(entries.shape)]
    main_axis = entries.shape.index(max(entries.shape))
    next_to = index_at[:main_axis] + [(index_at[main_axis] + 1) % entries.shape[main_axis]] + index_at[main_axis + 1:]
    return entries.at[tuple(index_at)].set(smallest).at[tuple(next_to)].set(top_value)


def block_scale(stream_key, shape, shards, least, high):
    loudness, own = 1.0, jax.random.fold_in(stream_key, 6)
    for dim, blocks in shards:
        steps = jnp.exp(jax.random.uniform(jax.random.fold_in(own, dim), (blocks,), jnp.float32, least / len(shards), high / len(shards)))
        loudness = loudness * jnp.repeat(steps, shape[dim] // blocks).reshape([-1 if axis == dim else 1 for axis in range(len(shape))])
    return loudness


def bell_draw(rng, shape, spread, reach, cuts=(), held_as=jnp.bfloat16):
    values = jax.random.normal(rng, shape, jnp.float32) * spread
    if len(cuts) > 0:
        values = block_scale(rng, shape, cuts, -0.22, 0.18) * values
    return jnp.clip(values, min=-reach, max=reach).astype(held_as)


def setup_inputs(seed: int = 0) -> dict:
    arg_keys = jax.random.split(jax.random.key(seed), 7)
    return {
        "probe_seeds": touch_ends(jax.random.randint(arg_keys[0], (PROBES,), 0, 32749), jax.random.fold_in(arg_keys[0], 1), 0, 32748).astype(jnp.int32),
        "leaf_inverse": draw_leaf_inverse(jax.random.fold_in(arg_keys[6], 71), 0),
        "leaf_update": bell_draw(arg_keys[2], (LEAVES, COLS, UPD * BLOCK), (4 * COLS) ** -0.5, 0.09375, ((0, 4), (1, 8))),
        "internal_inverse": draw_internal_inverse(jax.random.fold_in(arg_keys[6], 71), 0),
        "internal_update": bell_draw(arg_keys[4], (LEAVES, COLS, UPD * BLOCK), (4 * COLS) ** -0.5, 0.09375, ((0, 4), (1, 8))),
        "child_map": draw_child_map(jax.random.fold_in(arg_keys[6], 71), 0),
    }


HIGHEST = lax.Precision.HIGHEST


def probe_signs(seeds, node_id, columns):
    index = node_id * columns + jnp.arange(columns, dtype=jnp.int32)
    lower = index % 32749
    upper = index // 32749
    hashed = (lower * 30011 + upper * 7717 + seeds[:, None]) % 32749
    hashed = (hashed * hashed) % 32749
    hashed = (hashed * 21143 + lower) % 32749
    hashed = (hashed * hashed + upper) % 32749
    return (1 - 2 * ((hashed // 8) % 2)).astype(jnp.bfloat16)


def place_blocks(vectors, targets, front_blocks):
    onehot = (targets[:, :, None] == jnp.arange(front_blocks, dtype=jnp.int32)[None, None, :]).astype(jnp.float32)
    shaped = vectors.reshape(vectors.shape[0], vectors.shape[1], targets.shape[1], BLOCK)
    placed = jnp.einsum('npkb,nkt->nptb', shaped, onehot, precision=HIGHEST)
    return placed.reshape(vectors.shape[0], vectors.shape[1], front_blocks * BLOCK)


def pick_blocks(front_vector, targets, front_blocks):
    onehot = (targets[:, :, None] == jnp.arange(front_blocks, dtype=jnp.int32)[None, None, :]).astype(jnp.float32)
    shaped = front_vector.astype(jnp.float32).reshape(front_vector.shape[0], front_vector.shape[1], front_blocks, BLOCK)
    picked = jnp.einsum('nptb,nkt->npkb', shaped, onehot, precision=HIGHEST).astype(jnp.bfloat16)
    return picked.reshape(front_vector.shape[0], front_vector.shape[1], targets.shape[1] * BLOCK)


def apply_inverse(right_side, inverse):
    return jnp.einsum('npj,nij->npi', right_side.astype(jnp.float32), inverse.astype(jnp.float32))


def apply_transposed(right_side, inverse):
    return jnp.einsum('npi,nij->npj', right_side.astype(jnp.float32), inverse.astype(jnp.float32))


def push_update(solved, update):
    return jnp.einsum('npi,niu->npu', solved.astype(jnp.float32), update.astype(jnp.float32))


def pull_update(incoming, update):
    return jnp.einsum('npu,niu->npi', incoming.astype(jnp.float32), update.astype(jnp.float32))


def reference(probe_seeds, leaf_inverse, leaf_update, internal_inverse, internal_update, child_map):
    leaves = leaf_inverse.shape[0]
    columns = leaf_inverse.shape[1]
    col_blocks = columns // BLOCK
    upd_blocks = leaf_update.shape[2] // BLOCK
    front_blocks = col_blocks + upd_blocks
    probe_count = probe_seeds.shape[0]
    heights = leaves.bit_length() - 1
    node_ids = jnp.arange(leaves, dtype=jnp.int32)
    signer = jax.vmap(probe_signs, in_axes=(None, 0, None))
    leaf_signs = signer(probe_seeds, node_ids, columns)
    inner_signs = signer(probe_seeds, node_ids + leaves, columns)

    leaf_solved = apply_inverse(leaf_signs, leaf_inverse)
    leaf_sent = push_update(leaf_solved.astype(jnp.bfloat16), leaf_update)
    inner_solved = jnp.zeros((leaves, probe_count, columns), jnp.float32)
    inner_sent = jnp.zeros((leaves, probe_count, upd_blocks * BLOCK), jnp.float32)
    for height in range(1, heights + 1):
        half_span = 2 ** (height - 1)
        slot_ids = np.arange(half_span, leaves, 2 * half_span)
        rows = slot_ids - 1
        if height == 1:
            left_sent = leaf_sent[slot_ids - 1]
            right_sent = leaf_sent[slot_ids]
        else:
            distance = half_span // 2
            left_sent = inner_sent[slot_ids - distance]
            right_sent = inner_sent[slot_ids + distance]
        lists_now = child_map[rows]
        gathered = place_blocks(left_sent, lists_now[:, 0], front_blocks) + place_blocks(right_sent, lists_now[:, 1], front_blocks)
        residual = (inner_signs[slot_ids].astype(jnp.float32) - gathered[:, :, :columns]).astype(jnp.bfloat16)
        solved = apply_inverse(residual, internal_inverse[rows])
        sent = gathered[:, :, columns:] + push_update(solved.astype(jnp.bfloat16), internal_update[rows])
        inner_solved = inner_solved.at[slot_ids].set(solved)
        inner_sent = inner_sent.at[slot_ids].set(sent)

    inner_result = jnp.zeros((leaves, probe_count, columns), jnp.float32)
    inner_incoming = jnp.zeros((leaves, probe_count, upd_blocks * BLOCK), jnp.bfloat16)
    leaf_incoming = jnp.zeros((leaves, probe_count, upd_blocks * BLOCK), jnp.bfloat16)
    for height in range(heights, 0, -1):
        half_span = 2 ** (height - 1)
        slot_ids = np.arange(half_span, leaves, 2 * half_span)
        rows = slot_ids - 1
        incoming = inner_incoming[slot_ids]
        scaled = (inner_solved[slot_ids] - pull_update(incoming, internal_update[rows])).astype(jnp.bfloat16)
        solution = apply_transposed(scaled, internal_inverse[rows])
        inner_result = inner_result.at[rows].set(solution)
        front_vector = jnp.concatenate([solution.astype(jnp.bfloat16), incoming], axis=2)
        lists_now = child_map[rows]
        for_left = pick_blocks(front_vector, lists_now[:, 0], front_blocks)
        for_right = pick_blocks(front_vector, lists_now[:, 1], front_blocks)
        if height == 1:
            leaf_incoming = leaf_incoming.at[slot_ids - 1].set(for_left)
            leaf_incoming = leaf_incoming.at[slot_ids].set(for_right)
        else:
            distance = half_span // 2
            inner_incoming = inner_incoming.at[slot_ids - distance].set(for_left)
            inner_incoming = inner_incoming.at[slot_ids + distance].set(for_right)
    leaf_scaled = (leaf_solved - pull_update(leaf_incoming, leaf_update)).astype(jnp.bfloat16)
    leaf_result = apply_transposed(leaf_scaled, leaf_inverse)
    return leaf_result, inner_result
```

```python
import functools

import jax
import jax.numpy as jnp
from jax import lax
from jax.experimental import pallas as pl
from jax.experimental.pallas import tpu as pltpu
from jax.sharding import PartitionSpec as P

BLOCK = 64
LANES = 128


def probe_signs(seeds, node_id, columns):
    index = node_id * columns + jnp.arange(columns, dtype=jnp.int32)
    lower = index % 32749
    upper = index // 32749
    hashed = (lower * 30011 + upper * 7717 + seeds[:, None]) % 32749
    hashed = hashed * hashed % 32749
    hashed = (hashed * 21143 + lower) % 32749
    hashed = (hashed * hashed + upper) % 32749
    return (1 - 2 * (hashed // 8 % 2)).astype(jnp.bfloat16)


def times_transposed(left, right):
    return lax.dot_general(left, right, (((1,), (1,)), ((), ())), preferred_element_type=jnp.float32)


def times(left, right):
    return jnp.dot(left, right, preferred_element_type=jnp.float32)


def inverse_map(targets_of, wanted):
    source = jnp.arange(targets_of.shape[0], dtype=jnp.int32)
    hit = targets_of[None, :] == wanted[:, None]
    return jnp.max(jnp.where(hit, source[None, :], -1), axis=1)


def take_kernel(index_ref, values_ref, out_ref):
    tiles = out_ref.shape[1] // LANES
    rows = out_ref.shape[0]
    low = lax.broadcasted_iota(jnp.int32, (rows, LANES), 1) < BLOCK

    def half(block, side):
        at = jnp.maximum(block, 0)
        start = pl.multiple_of(at // 2 * LANES, LANES)
        tile = values_ref[:, pl.ds(start, LANES)].astype(jnp.float32)
        turned = pltpu.roll(tile, BLOCK, 1)
        tile = jnp.where(at % 2 == side, tile, turned)
        return jnp.where(block >= 0, tile, 0.0)

    def step(tile, carry):
        left = half(index_ref[2 * tile], 0)
        right = half(index_ref[2 * tile + 1], 1)
        start = pl.multiple_of(tile * LANES, LANES)
        out_ref[:, pl.ds(start, LANES)] = jnp.where(low, left, right).astype(out_ref.dtype)
        return carry

    lax.fori_loop(0, tiles, step, 0)


def take_blocks(values, index, name):
    rows = values.shape[0]
    width = index.shape[0] * BLOCK
    return pl.pallas_call(
        take_kernel,
        out_shape=jax.ShapeDtypeStruct((rows, width), values.dtype),
        in_specs=[
            pl.BlockSpec(memory_space=pltpu.SMEM),
            pl.BlockSpec(memory_space=pltpu.VMEM),
        ],
        out_specs=pl.BlockSpec(memory_space=pltpu.VMEM),
        name=name,
    )(index, values)


def shards(probe_seeds, leaf_inverse, leaf_update, internal_inverse, internal_update, child_map):
    leaves = lax.axis_size("leaf")
    fronts = lax.axis_size("front")
    chips = fronts // 2
    position = lax.axis_index("leaf")
    member = lax.axis_index("front")
    core = member % 2
    leaf_inv, leaf_upd = leaf_inverse[0], leaf_update[0]
    inner_inv, inner_upd = internal_inverse[0], internal_update[0]
    own_width, columns = leaf_inv.shape
    col_blocks = columns // BLOCK
    bits = chips.bit_length() - 1

    def both(pairs_leaf, pairs_front):
        return [(a * fronts + c, b * fronts + d) for a, b in pairs_leaf for c, d in pairs_front]

    every_leaf = [(p, p) for p in range(leaves)]
    every_front = [(f, f) for f in range(fronts)]
    core_one = [(2 * c + 1, 2 * c + 1) for c in range(chips)]

    def send(value, pairs):
        return lax.ppermute(value, ("leaf", "front"), pairs)

    def to_core_one(value):
        return send(value, both(every_leaf, [(2 * c, 2 * c + 1) for c in range(chips)]))

    def to_core_zero(value):
        return send(value, both(every_leaf, [(2 * c + 1, 2 * c) for c in range(chips)]))

    def over_chip(value, bit):
        step = 1 << bit
        return send(
            value, both(every_leaf, [(2 * c + 1, 2 * (c ^ step) + 1) for c in range(chips)])
        )

    def over_leaf(value, step, fronts_used=core_one):
        return send(value, both([(p, p ^ step) for p in range(leaves)], fronts_used))

    def added(total, move):
        return total + move(total.astype(jnp.bfloat16)).astype(jnp.float32)

    def chip_sum(total):
        for bit in range(bits):
            total = added(total, functools.partial(over_chip, bit=bit))
        return total

    odd = position % 2 == 1
    upper = position >= 2
    own_map = child_map[0]
    beside = over_leaf(own_map, 1, every_front)
    slot_map = jnp.where(odd, beside[1], own_map[0])
    low_root = jnp.where(odd, own_map, beside)
    across = send(low_root, both([(0, 2), (1, 3)], every_front))
    root_map = jnp.where(upper, across[1], low_root[0])
    wanted = jnp.arange(col_blocks, dtype=jnp.int32)
    blocks_a = inverse_map(slot_map, wanted)
    blocks_c = inverse_map(root_map, wanted)
    blocks_b = inverse_map(slot_map, jnp.where(blocks_c >= 0, col_blocks + blocks_c, -2))

    leaf_signs = probe_signs(probe_seeds, position, columns)
    leaf_solved = times_transposed(leaf_signs, leaf_inv)
    leaf_sent = times(leaf_solved.astype(jnp.bfloat16), leaf_upd)
    part_a = take_blocks(leaf_sent, blocks_a, "take_a")
    total = added(part_a, to_core_one)
    total = chip_sum(total)
    total = added(total, functools.partial(over_leaf, step=1))

    inv_beside = over_leaf(inner_inv, 1, every_front)
    slot_inv = jnp.where(odd, inv_beside, inner_inv)
    low_root_inv = jnp.where(odd, inner_inv, inv_beside)
    inv_across = send(low_root_inv, both([(0, 2), (1, 3)], every_front))
    root_inv = jnp.where(upper, inv_across, low_root_inv)
    own_c = take_blocks(inner_upd, blocks_c, "take_c")
    c_beside = send(own_c, both([(p, p + 1) for p in range(0, leaves, 2)], every_front))
    slot_c = jnp.where(odd, c_beside, own_c)

    def chip_rows(value, axis=0):
        return jnp.concatenate([to_core_one(value), value], axis=axis)

    slot_inv, slot_c, root_inv = chip_rows(slot_inv), chip_rows(slot_c), chip_rows(root_inv)
    leaf_a = chip_rows(take_blocks(leaf_upd, blocks_a, "take_leaf_a"))
    leaf_b = chip_rows(take_blocks(leaf_upd, blocks_b, "take_leaf_b"))
    leaf_rows = chip_rows(leaf_inv)
    leaf_y = chip_rows(leaf_solved, 1)

    part_b = take_blocks(leaf_sent, blocks_b, "take_b")
    total_b = added(part_b, to_core_one)
    total_b = added(total_b, functools.partial(over_leaf, step=1))

    slot_signs = probe_signs(probe_seeds, leaves + position // 2 * 2 + 1, columns)
    residual = (slot_signs.astype(jnp.float32) - total).astype(jnp.bfloat16)
    slot_y = times_transposed(residual, slot_inv)
    total = times(slot_y.astype(jnp.bfloat16), slot_c) + total_b
    total = chip_sum(total)
    total = added(total, functools.partial(over_leaf, step=2))

    root_signs = probe_signs(probe_seeds, leaves + leaves // 2, columns)
    residual = (root_signs.astype(jnp.float32) - total).astype(jnp.bfloat16)
    root_y = times_transposed(residual, root_inv)
    root_x = chip_sum(times(root_y.astype(jnp.bfloat16), root_inv))
    root_u = root_x.astype(jnp.bfloat16)

    scaled = (slot_y - times_transposed(root_u, slot_c)).astype(jnp.bfloat16)
    slot_x = chip_sum(times(scaled, slot_inv))
    slot_u = slot_x.astype(jnp.bfloat16)

    pulled = times_transposed(slot_u, leaf_a) + times_transposed(root_u, leaf_b)
    scaled = (leaf_y - pulled).astype(jnp.bfloat16)
    part = times(scaled, leaf_rows)
    chip = member // 2
    for bit in reversed(range(bits)):
        half = part.shape[1] // 2
        is_high = (chip >> bit) % 2 == 1
        keep = jnp.where(is_high, part[:, half:], part[:, :half])
        give = jnp.where(is_high, part[:, :half], part[:, half:]).astype(jnp.bfloat16)
        part = keep + over_chip(give, bit).astype(jnp.float32)

    def own_block(value):
        given = to_core_zero(value[:, :own_width].astype(jnp.bfloat16)).astype(jnp.float32)
        return jnp.where(core == 1, value[:, own_width:], given)

    leaf_result = own_block(part)
    inner = jnp.where(position == leaves // 2 - 1, root_x, slot_x)
    inner = jnp.where(position == leaves - 1, 0.0, inner)
    inner = lax.dynamic_slice_in_dim(inner, chip * 2 * own_width, 2 * own_width, 1)
    inner_result = own_block(inner)
    return (leaf_result[None], inner_result[None])


def solution(mesh):
    return jax.shard_map(
        shards,
        mesh=mesh,
        in_specs=(
            P(),
            P("leaf", "front", None),
            P("leaf", "front", None),
            P("leaf", "front", None),
            P("leaf", "front", None),
            P("leaf", None, None),
        ),
        out_specs=(P("leaf", None, "front"), P("leaf", None, "front")),
        check_vma=False,
    )
```

```python
import jax
import jax.numpy as jnp
from jax import lax
from jax.experimental import pallas as pl
from jax.experimental.pallas import tpu as pltpu
from jax.sharding import PartitionSpec as P

BLOCK = 64
LANES = 128


def probe_signs(seeds, node_id, columns):
    index = node_id * columns + jnp.arange(columns, dtype=jnp.int32)
    lower = index % 32749
    upper = index // 32749
    hashed = (lower * 30011 + upper * 7717 + seeds[:, None]) % 32749
    hashed = hashed * hashed % 32749
    hashed = (hashed * 21143 + lower) % 32749
    hashed = (hashed * hashed + upper) % 32749
    return (1 - 2 * (hashed // 8 % 2)).astype(jnp.bfloat16)


def times_transposed(left, right):
    return lax.dot_general(left, right, (((1,), (1,)), ((), ())), preferred_element_type=jnp.float32)


def times(left, right):
    return jnp.dot(left, right, preferred_element_type=jnp.float32)


def inverse_map(targets_of, wanted):
    source = jnp.arange(targets_of.shape[0], dtype=jnp.int32)
    hit = targets_of[None, :] == wanted[:, None]
    return jnp.max(jnp.where(hit, source[None, :], -1), axis=1)


def take_kernel(index_ref, values_ref, out_ref):
    tiles = out_ref.shape[1] // LANES
    rows = out_ref.shape[0]
    low = lax.broadcasted_iota(jnp.int32, (rows, LANES), 1) < BLOCK

    def half(block, side):
        at = jnp.maximum(block, 0)
        start = pl.multiple_of(at // 2 * LANES, LANES)
        tile = values_ref[:, pl.ds(start, LANES)].astype(jnp.float32)
        turned = pltpu.roll(tile, BLOCK, 1)
        tile = jnp.where(at % 2 == side, tile, turned)
        return jnp.where(block >= 0, tile, 0.0)

    def step(tile, carry):
        left = half(index_ref[2 * tile], 0)
        right = half(index_ref[2 * tile + 1], 1)
        start = pl.multiple_of(tile * LANES, LANES)
        out_ref[:, pl.ds(start, LANES)] = jnp.where(low, left, right).astype(out_ref.dtype)
        return carry

    if tiles <= 16:
        for tile in range(tiles):
            step(tile, 0)
    else:
        lax.fori_loop(0, tiles, step, 0)


def take_blocks(values, index, name):
    rows = values.shape[0]
    width = index.shape[0] * BLOCK
    size = values.dtype.itemsize * rows * (values.shape[1] + width)
    return pl.pallas_call(
        take_kernel,
        out_shape=jax.ShapeDtypeStruct((rows, width), values.dtype),
        in_specs=[
            pl.BlockSpec(memory_space=pltpu.SMEM),
            pl.BlockSpec(memory_space=pltpu.VMEM),
        ],
        out_specs=pl.BlockSpec(memory_space=pltpu.VMEM),
        compiler_params=pltpu.CompilerParams(vmem_limit_bytes=size + (2 << 20)),
        cost_estimate=pl.CostEstimate(flops=0, bytes_accessed=size, transcendentals=0),
        name=name,
    )(index, values)


def shards(probe_seeds, leaf_inverse, leaf_update, internal_inverse, internal_update, child_map):
    leaves = lax.axis_size("leaf")
    fronts = lax.axis_size("front")
    chips = fronts // 2
    position = lax.axis_index("leaf")
    member = lax.axis_index("front")
    chip, core = member // 2, member % 2
    on_one = core == 1
    leaf_inv, leaf_upd = leaf_inverse[0], leaf_update[0]
    inner_inv, inner_upd = internal_inverse[0], internal_update[0]
    own_width, columns = leaf_inv.shape
    chip_width = 2 * own_width
    col_blocks = columns // BLOCK

    def swap(value):
        return lax.ppermute(value, "front", [(f, f ^ 1) for f in range(fronts)])

    def over_leaf(value, step):
        return lax.ppermute(value, "leaf", [(p, p ^ step) for p in range(leaves)])

    def over_chip(value, step, aside):
        pairs = []
        for p in range(leaves):
            for c in range(chips):
                pairs.append((p * fronts + 2 * c, (p ^ aside) * fronts + 2 * c))
                pairs.append((p * fronts + 2 * c + 1, p * fronts + 2 * (c ^ step) + 1))
        return lax.ppermute(value, ("leaf", "front"), pairs)

    def groups():
        base = 1
        while base < chips:
            count = 4 if base * 4 <= chips else 2
            yield [(base * k, (0, 3, 1, 2)[k]) for k in range(1, count)]
            base *= count

    def chip_sum(total):
        for steps in groups():
            sent = total.astype(jnp.bfloat16)
            for got in [over_chip(sent, step, aside) for step, aside in steps]:
                total = total + got.astype(jnp.float32)
        return total

    def chip_scatter(total):
        for steps in groups():
            count = len(steps) + 1
            base = steps[0][0]
            width = total.shape[1] // (chips // base)
            parts = total.reshape(total.shape[0], chips // base // count, count, width)
            digit = chip // base % count

            def block(at):
                return lax.dynamic_index_in_dim(parts, at, 2, keepdims=False).reshape(total.shape[0], -1)

            kept = block(digit)
            for k, (step, aside) in enumerate(steps, 1):
                given = block(digit ^ k).astype(jnp.bfloat16)
                kept = kept + over_chip(given, step, aside).astype(jnp.float32)
            total = kept
        return total

    odd = position % 2 == 1
    upper = position >= 2
    own_map = child_map[0]
    at_one, at_two, at_three = (over_leaf(own_map, step) for step in (1, 2, 3))
    slot_map = jnp.where(odd, at_one[1], own_map[0])
    root_map = jnp.where(
        upper, jnp.where(odd, at_two[1], at_three[1]), jnp.where(odd, own_map[0], at_one[0])
    )
    wanted = jnp.arange(col_blocks, dtype=jnp.int32)
    blocks_a = inverse_map(slot_map, wanted)
    blocks_c = inverse_map(root_map, wanted)
    blocks_b = inverse_map(slot_map, jnp.where(blocks_c >= 0, col_blocks + blocks_c, -2))

    leaf_signs = probe_signs(probe_seeds, position, columns)
    leaf_solved = times_transposed(leaf_signs, leaf_inv)
    leaf_sent = times(leaf_solved.astype(jnp.bfloat16), leaf_upd)
    leaf_sent = leaf_sent + swap(leaf_sent.astype(jnp.bfloat16)).astype(jnp.float32)
    part = take_blocks(leaf_sent, jnp.where(on_one, blocks_a, blocks_b), "take_sent")
    total = chip_sum(part)
    total = total + over_leaf(total.astype(jnp.bfloat16), 1).astype(jnp.float32)

    root_part = part + over_leaf(part.astype(jnp.bfloat16), 1).astype(jnp.float32)
    root_part = swap(root_part.astype(jnp.bfloat16)).astype(jnp.float32)

    inv_beside = over_leaf(inner_inv, 1)
    slot_inv = jnp.where(odd, inv_beside, inner_inv)
    root_inv = jnp.where(odd, inner_inv, inv_beside)
    root_inv = jnp.where(upper, over_leaf(root_inv, 2), root_inv)
    own_c = take_blocks(inner_upd, blocks_c, "take_inner")
    slot_c = jnp.where(odd, over_leaf(own_c, 1), own_c)
    leaf_ab = take_blocks(leaf_upd, jnp.concatenate([blocks_a, blocks_b]), "take_leaf")

    def chip_rows(value, axis=0):
        return jnp.concatenate([swap(value), value], axis=axis)

    slot_inv, slot_c, root_inv = chip_rows(slot_inv), chip_rows(slot_c), chip_rows(root_inv)
    leaf_ab, leaf_rows = chip_rows(leaf_ab), chip_rows(leaf_inv)
    leaf_y = chip_rows(leaf_solved, 1)

    slot_signs = probe_signs(probe_seeds, leaves + position // 2 * 2 + 1, columns)
    residual = (slot_signs.astype(jnp.float32) - total).astype(jnp.bfloat16)
    slot_y = times_transposed(residual, slot_inv)
    total = chip_sum(times(slot_y.astype(jnp.bfloat16), slot_c) + root_part)
    total = total + over_leaf(total.astype(jnp.bfloat16), 2).astype(jnp.float32)

    root_signs = probe_signs(probe_seeds, leaves + leaves // 2, columns)
    residual = (root_signs.astype(jnp.float32) - total).astype(jnp.bfloat16)
    root_y = times_transposed(residual, root_inv)
    root_x = chip_sum(times(root_y.astype(jnp.bfloat16), root_inv))
    root_u = root_x.astype(jnp.bfloat16)

    scaled = (slot_y - times_transposed(root_u, slot_c)).astype(jnp.bfloat16)
    slot_x = chip_sum(times(scaled, slot_inv))
    slot_u = slot_x.astype(jnp.bfloat16)

    pulled = times_transposed(jnp.concatenate([slot_u, root_u], axis=1), leaf_ab)
    scaled = (leaf_y - pulled).astype(jnp.bfloat16)
    part = chip_scatter(times(scaled, leaf_rows))

    def own_block(value):
        return jnp.where(on_one, value[:, own_width:], swap(value[:, :own_width]))

    inner = jnp.where(position == leaves // 2 - 1, root_x, slot_x)
    inner = jnp.where(position == leaves - 1, 0.0, inner)
    inner = lax.dynamic_slice_in_dim(inner, chip * chip_width, chip_width, 1)
    return (own_block(part)[None], own_block(inner)[None])


def solution(mesh):
    return jax.shard_map(
        shards,
        mesh=mesh,
        in_specs=(
            P(),
            P("leaf", "front", None),
            P("leaf", "front", None),
            P("leaf", "front", None),
            P("leaf", "front", None),
            P("leaf", None, None),
        ),
        out_specs=(P("leaf", None, "front"), P("leaf", None, "front")),
        check_vma=False,
    )
```
